32 devices in a mesh: row: 4 (over y, core), col: 8 (over z, x).
Axes of the slice: x: 2, y: 2, z: 4, core: 2. Of those that a mesh axis runs over, the one named last changes fastest.
Arguments:
- ancestor_inverse: float32 [1024, 1024], P('row', 'col'), may hold values from -6 to 6
- pattern: int32 [8, 8], replicated, may hold values 0 or 1
- listed: int32 [2, 4], replicated, may hold values from 0 to 7, as said below
- panels: float32 [2, 1024, 512], P(None, ('col', 'row')), may hold values from -0.1875 to 0.1875
- parent_panels: float32 [1, 512, 512], replicated, may hold values from -0.25 to 0.25
- diag_inverse: float32 [2, 512, 512], P(None, 'row', 'col'), may hold values from -6 to 6
Outputs:
- upper_blocks: float32 [2, 1024, 512], P(None, ('col', 'row'))
- diagonal_blocks: float32 [2, 512, 512], P(None, 'row', 'col')
The draws below stay inside these ranges and needn't reach their ends.
Inputs may be any that keep to these rules, and one draw needn't show every extreme that they name: Each row of listed names 4 different blocks.
All inputs are finite; a program needn't handle non-finite values.
Results may differ from the reference program's by a relative error of at most 0.00011.
Values sent between devices are 32-bit elements; how exact they have to be, the bound alone decides.
No kernel may reach another device: no remote copies, remote signals or barrier semaphores. Data moves between devices by JAX's collectives and lax.ppermute only.
A program may use at most 64 MiB of HBM per device.

```python
import jax
import jax.numpy as jnp
from jax import lax

W = 512
BLK = 128
SUPER = 2
NANC = 1024
LISTED = 4


def draw_listed(key, part):
    chosen = []
    for supernode in range(SUPER):
        order = jax.random.permutation(jax.random.fold_in(key, 17 + supernode), NANC // BLK)
        chosen.append(order[:LISTED])
    return jnp.stack(chosen).astype(jnp.int32)


def set_ends(entries, stream_key, least, top_value):
    shape = entries.shape
    spot = [jax.random.randint(jax.random.fold_in(stream_key, axis), (), 0, shape[axis]) for axis in range(len(shape))]
    entries = entries.at[tuple(spot)].set(least)
    longest = shape.index(max(shape))
    spot[longest] = (spot[longest] + 1) % shape[longest]
    return entries.at[tuple(spot)].set(top_value)


def shard_levels(own_key, extent, cuts, low, top_value):
    def one(dim, shards_of):
        steps = jax.random.uniform(jax.random.fold_in(jax.random.fold_in(own_key, 6), dim), (shards_of,), jnp.float32, low / len(cuts), top_value / len(cuts))
        return jnp.repeat(jnp.exp(steps), extent[dim] // shards_of).reshape((-1,) + (1,) * (len(extent) - dim - 1))

    loudness = one(*cuts[0])
    for cut in cuts[1:]:
        loudness = loudness * one(*cut)
    return loudness


def gaussian(stream_key, extent, spread, reach, cuts=(), held_as=jnp.bfloat16):
    values = jax.random.normal(stream_key, extent, jnp.float32) * spread
    if len(cuts) > 0:
        values = shard_levels(stream_key, extent, cuts, -0.22, 0.18) * values
    return jnp.clip(values, min=-reach, max=reach).astype(held_as)


def setup_inputs(seed: int = 0) -> dict:
    keys = jax.random.split(jax.random.key(seed), 7)
    ancestor_inverse = gaussian(keys[0], (NANC, NANC), 1.0, 6.0, ((0, 4), (1, 8)), jnp.float32)
    pattern = set_ends((jax.random.randint(keys[1], (NANC // BLK, NANC // BLK), 0, 4) < 3).astype(jnp.int32), jax.random.fold_in(keys[1], 1), 0, 1)
    listed = draw_listed(jax.random.fold_in(keys[6], 71), 0)
    panels = gaussian(keys[3], (SUPER, NANC, W), NANC ** -0.5, 0.1875, ((1, 32),), jnp.float32)
    parent_panels = gaussian(keys[4], (SUPER - 1, W, W), W ** -0.5, 0.25, (), jnp.float32)
    diag_inverse = gaussian(keys[5], (SUPER, W, W), 1.0, 6.0, ((1, 4), (2, 8)), jnp.float32)
    return dict(ancestor_inverse=ancestor_inverse, pattern=pattern, listed=listed, panels=panels, parent_panels=parent_panels, diag_inverse=diag_inverse)


def contract_rows(left, right):
    return lax.dot_general(left, right, (((0,), (0,)), ((), ())), precision=lax.Precision.HIGHEST, preferred_element_type=jnp.float32)


def reference(ancestor_inverse, pattern, listed, panels, parent_panels, diag_inverse):
    highest = lax.Precision.HIGHEST
    blocks = NANC // BLK
    masked = (ancestor_inverse.reshape(blocks, BLK, blocks, BLK) * pattern.astype(jnp.float32)[:, None, :, None]).reshape(NANC, NANC)
    block_ids = jnp.arange(blocks, dtype=jnp.int32)
    listed_flags = jnp.any(listed[:, :, None] == block_ids[None, None, :], axis=1).astype(jnp.float32)
    row_keep = jnp.repeat(listed_flags, BLK, axis=1)
    uppers = []
    diagonals = []
    for supernode in range(SUPER):
        kept_panel = panels[supernode] * row_keep[supernode][:, None]
        column_sum = contract_rows(masked, kept_panel)
        if supernode > 0:
            parent_link = parent_panels[supernode - 1]
            chained = jnp.dot(uppers[-1], parent_link, precision=highest, preferred_element_type=jnp.float32)
            column_sum = column_sum + chained
        upper_part = -column_sum * row_keep[supernode][:, None]
        diagonal = diag_inverse[supernode] - contract_rows(kept_panel, upper_part)
        if supernode > 0:
            carried = jnp.dot(diagonals[-1], parent_link, precision=highest, preferred_element_type=jnp.float32)
            diagonal = diagonal + contract_rows(chained, kept_panel) + contract_rows(parent_link, carried)
        uppers.append(upper_part)
        diagonals.append(diagonal)
    return jnp.stack(uppers), jnp.stack(diagonals)
```

```python
import jax
import jax.numpy as jnp
from jax import lax
from jax.sharding import PartitionSpec as P

BLK = 128


def swap(value, axis, distance):
    size = lax.axis_size(axis)
    return lax.ppermute(value, axis, [(i, i ^ distance) for i in range(size)])


def gather_relative(value, axis):
    parts = value[None]
    distance = lax.axis_size(axis) // 2
    while distance:
        both = jnp.stack([parts, swap(parts, axis, distance)], axis=1)
        parts = both.reshape((-1,) + value.shape)
        distance //= 2
    return parts


def natural(parts, index):
    return [
        lax.dynamic_index_in_dim(parts, index ^ j, 0, keepdims=False)
        for j in range(parts.shape[0])
    ]


def dot(left, right, left_dim=1, right_dim=0):
    return lax.dot_general(
        left,
        right,
        (((left_dim,), (right_dim,)), ((), ())),
        precision=lax.Precision.HIGH,
        preferred_element_type=jnp.float32,
    )


def local(ancestor_inverse, pattern, listed, panels, parent_panels, diag_inverse):
    rows_here, cols_here = ancestor_inverse.shape
    row_count = lax.axis_size("row")
    col_count = lax.axis_size("col")
    row_index = lax.axis_index("row")
    col_index = lax.axis_index("col")
    super_count, shard_rows, width = panels.shape
    tile_rows = width // row_count
    tile_cols = width // col_count
    group_rows = shard_rows * row_count
    blocks = pattern.shape[0]
    link = parent_panels[0]

    raw = jnp.concatenate(natural(gather_relative(panels, "row"), row_index), axis=1)
    block_ids = jnp.arange(blocks, dtype=jnp.int32)
    flags = jnp.any(listed[:, :, None] == block_ids[None, None, :], axis=1)
    own_rows = col_index * group_rows + jnp.arange(group_rows, dtype=jnp.int32)
    onehot = (own_rows[:, None] // BLK) == block_ids[None, :]
    keep = jnp.any(flags[:, None, :] & onehot[None, :, :], axis=2).astype(jnp.float32)
    kept = raw * keep[:, :, None]

    tile = gather_relative(ancestor_inverse, "row")
    ratio = rows_here // group_rows
    first = col_index * cols_here
    row_block = jnp.arange(row_count * rows_here, dtype=jnp.int32) // BLK
    col_block = (first + jnp.arange(cols_here, dtype=jnp.int32)) // BLK
    rows_mask = ((row_block[:, None] == block_ids[None, :]).astype(jnp.float32)) @ (
        pattern.astype(jnp.float32)
    )
    mask = rows_mask @ (col_block[:, None] == block_ids[None, :]).astype(jnp.float32).T
    mask = mask.reshape(col_count, group_rows, cols_here)

    mine = jnp.concatenate(
        [
            lax.dynamic_slice_in_dim(kept[s], row_index * tile_rows, tile_rows, 1)
            for s in range(super_count)
        ],
        axis=1,
    )
    pieces = {0: mine}
    for j in range(2, col_count, 2):
        pieces[j] = swap(mine, "col", j)
    for j in range(0, col_count, 2):
        pieces[j + 1] = swap(pieces[j], "col", 1)
    total = None
    for j in range(col_count):
        source = col_index ^ j
        held = lax.dynamic_index_in_dim(
            tile.reshape(row_count, ratio, group_rows, cols_here),
            row_index ^ (source // ratio),
            0,
            keepdims=False,
        )
        held = lax.dynamic_index_in_dim(held, source % ratio, 0, keepdims=False)
        held = held * lax.dynamic_index_in_dim(mask, source, 0, keepdims=False)
        term = dot(held, pieces[j], 0, 0)
        total = term if total is None else total + term

    sums = natural(gather_relative(total, "row"), row_index)
    sums = [
        jnp.concatenate([part[:, s * tile_rows : (s + 1) * tile_rows] for part in sums], axis=1)
        for s in range(super_count)
    ]

    def band(value):
        return lax.dynamic_slice_in_dim(value, row_index * tile_rows, tile_rows, 1)

    diag_parts = natural(gather_relative(diag_inverse[:-1], "row"), row_index)
    uppers = []
    partials = []
    left_prior = None
    for s in range(super_count):
        column_sum = sums[s]
        if s > 0:
            parent = parent_panels[s - 1]
            chained = dot(uppers[-1], parent)
            column_sum = column_sum + chained
        upper = -column_sum * keep[s][:, None]
        rights = [upper]
        lefts = [-band(kept[s])]
        if s > 0:
            rights += [kept[s], chained]
            lefts += [band(chained), -dot(kept[s - 1], band(parent))]
            diag_cols = jnp.concatenate([part[s - 1] for part in diag_parts], axis=0)
            rights.append(
                lax.dynamic_slice_in_dim(parent, col_index * tile_cols, tile_cols, 0)
            )
            lefts.append(dot(diag_cols, band(parent), 0, 0))
        uppers.append(upper)
        partials.append(
            dot(jnp.concatenate(rights, axis=0), jnp.concatenate(lefts, axis=0), 0, 0)
        )

    half = jnp.stack(partials).reshape(super_count, col_count // 2, 2, tile_cols, tile_rows)
    low = col_index % 2
    near = lax.dynamic_index_in_dim(half, low, 2, keepdims=False) + swap(
        lax.dynamic_index_in_dim(half, 1 - low, 2, keepdims=False), "col", 1
    )
    high = col_index // 2
    reduced = lax.dynamic_index_in_dim(near, high, 1, keepdims=False)
    for j in range(2, col_count, 2):
        reduced = reduced + swap(
            lax.dynamic_index_in_dim(near, high ^ (j // 2), 1, keepdims=False), "col", j
        )
    diagonals = diag_inverse + jnp.swapaxes(reduced, 1, 2)
    own = [
        lax.dynamic_slice_in_dim(upper, row_index * shard_rows, shard_rows, 0)
        for upper in uppers
    ]
    return jnp.stack(own), diagonals


def solution(mesh):
    return jax.shard_map(
        local,
        mesh=mesh,
        in_specs=(
            P("row", "col"),
            P(),
            P(),
            P(None, ("col", "row"), None),
            P(),
            P(None, "row", "col"),
        ),
        out_specs=(P(None, ("col", "row"), None), P(None, "row", "col")),
        check_vma=False,
    )
```

```python
import jax
import jax.numpy as jnp
from jax import lax
from jax.sharding import PartitionSpec as P


BLK = 128


def swap(value, row_step, col_step):
    rows = lax.axis_size("row")
    cols = lax.axis_size("col")
    if col_step == 0:
        return lax.ppermute(value, "row", [(i, i ^ row_step) for i in range(rows)])
    if row_step == 0:
        return lax.ppermute(value, "col", [(i, i ^ col_step) for i in range(cols)])
    pairs = [
        (row * cols + col, (row ^ row_step) * cols + (col ^ col_step))
        for row in range(rows)
        for col in range(cols)
    ]
    return lax.ppermute(value, ("row", "col"), pairs)


def join(parts, other):
    return jnp.stack([parts, other], axis=1).reshape((-1,) + parts.shape[1:])


def after(value, *others):
    return lax.optimization_barrier((value,) + others)[1:]


def direct_gather(value):
    rows = lax.axis_size("row")
    far = [[swap(value, j, k) if j or k else value for k in range(2)] for j in range(0, rows, 2)]
    far = jnp.stack([jnp.stack(pair) for pair in far])
    return join(far, swap(far, 1, 0))


def rows_first(value):
    rows = lax.axis_size("row")
    far = value[None]
    step = rows // 2
    while step > 1:
        far = join(far, swap(far, step, 0))
        step //= 2
    far = jnp.stack([far, swap(far, 0, 1)], axis=1)
    return join(far, swap(far, 1, 0))


def column_first(value):
    rows = lax.axis_size("row")
    far = jnp.stack([value, swap(value, 0, 1)])[None]
    step = rows // 2
    while step > 1:
        far = join(far, swap(far, step, 0))
        step //= 2
    return join(far, swap(far, 1, 0))


def pick(value, *index):
    sizes = (1,) * len(index) + value.shape[len(index) :]
    start = tuple(index) + (0,) * (value.ndim - len(index))
    return lax.dynamic_slice(value, start, sizes).reshape(value.shape[len(index) :])


def dot(left, right, left_dim=1, right_dim=0):
    return lax.dot_general(
        left,
        right,
        (((left_dim,), (right_dim,)), ((), ())),
        precision=lax.Precision.HIGH,
        preferred_element_type=jnp.float32,
    )


def local(ancestor_inverse, pattern, listed, panels, parent_panels, diag_inverse):
    rows_here, cols_here = ancestor_inverse.shape
    row_count = lax.axis_size("row")
    col_count = lax.axis_size("col")
    row_index = lax.axis_index("row")
    col_index = lax.axis_index("col")
    low = col_index % 2
    high = col_index // 2
    planes = col_count // 2
    super_count, shard_rows, width = panels.shape
    tile_rows = width // row_count
    tile_cols = width // col_count
    group_rows = row_count * shard_rows
    plane_rows = 2 * group_rows
    blocks = pattern.shape[0]
    assert super_count == 2 and planes == row_count and rows_here == plane_rows
    assert group_rows == cols_here == BLK and blocks == col_count
    assert 2 * shard_rows == tile_cols
    members = [
        [(2 * plane + near) * row_count + row for near in range(2) for row in range(row_count)]
        for plane in range(planes)
    ]

    held = rows_first(ancestor_inverse)

    shares = jnp.swapaxes(panels.reshape(2, shard_rows, row_count, tile_rows), 1, 2)
    shares = shares.reshape(2 * row_count, shard_rows, tile_rows)
    piece = lax.all_to_all(
        shares, ("col", "row"), 0, 0, tiled=True, axis_index_groups=members
    ).reshape(plane_rows, tile_rows)

    pieces = {0: piece}
    step = planes // 2
    while step:
        for j in list(pieces):
            pieces[j ^ step] = swap(pieces[j], 0, 2 * step)
        step //= 2
    pattern, listed, link = after(piece, pattern, listed, parent_panels[0])

    block_ids = jnp.arange(blocks, dtype=jnp.int32)
    flags = jnp.any(listed[:, :, None] == block_ids[None, None, :], axis=1).astype(jnp.float32)
    seen = lax.dynamic_slice_in_dim(pattern, 2 * high, 2, 1).astype(jnp.float32)
    seen = (seen * pick(flags, low)[:, None]).reshape(planes, 2, 2)
    total = None
    for j in sorted(pieces, key=lambda j: (bin(j).count("1"), -j)):
        source = high ^ j
        weights = [
            pick(held, row_index ^ source, low ^ near).reshape(2, BLK, cols_here)
            * pick(seen, source)[:, near][:, None, None]
            for near in range(2)
        ]
        weights = jnp.concatenate([w.reshape(plane_rows, cols_here) for w in weights], axis=1)
        term = dot(weights, pieces[j], 0, 0)
        total = term if total is None else total + term

    keep = lax.dynamic_slice_in_dim(flags, 2 * high, 2, 1)
    keep = jnp.repeat(keep, BLK, axis=1)[:, :, None]
    raw = jnp.concatenate([panels.reshape(2 * shard_rows, width), diag_inverse[0].T], axis=1)
    raw = column_first(raw)
    raw = jnp.stack([pick(raw, row_index ^ r, low ^ k) for k in range(2) for r in range(row_count)])
    diag_rows = raw[:, :, width:].reshape(2, row_count, tile_cols, tile_rows)
    diag_rows = jnp.concatenate(
        [diag_rows[:, r].reshape(2 * tile_cols, tile_rows) for r in range(row_count)], axis=1
    )
    kept_all = [
        raw[:, s * shard_rows : (s + 1) * shard_rows, :width].reshape(plane_rows, width) * keep[s]
        for s in range(2)
    ]

    def band(value):
        return lax.dynamic_slice_in_dim(value, row_index * tile_rows, tile_rows, 1)

    kept_own = [band(value) for value in kept_all]
    link_own = band(link)
    moved = dot(kept_all[0], link_own)
    link_rows = lax.dynamic_slice_in_dim(link, high * 2 * tile_cols, 2 * tile_cols, 0)
    base = dot(dot(diag_rows, link_own), link_rows, 0, 0)

    sums = direct_gather(total)
    sums = [
        jnp.concatenate([pick(sums, row_index ^ r, low ^ s) for r in range(row_count)], axis=1)
        for s in range(2)
    ]
    upper = -sums[0] * keep[0]
    chained = dot(upper, link)
    upper_next = -(sums[1] + chained) * keep[1]
    tiles = [
        dot(-kept_own[0], upper, 0, 0),
        base
        + dot(-kept_own[1], upper_next, 0, 0)
        + dot(band(chained), kept_all[1], 0, 0)
        + dot(-moved, chained, 0, 0),
    ]
    tiles = jnp.stack([tile.T for tile in tiles]).reshape(2, planes, 2, tile_cols, tile_rows)
    tiles = lax.dynamic_index_in_dim(tiles, low, 2, keepdims=False)
    reduced = lax.dynamic_index_in_dim(tiles, high, 1, keepdims=False)
    for j in range(1, planes):
        reduced = reduced + swap(
            lax.dynamic_index_in_dim(tiles, high ^ j, 1, keepdims=False), 0, 2 * j
        )
    diagonals = diag_inverse + jnp.swapaxes(reduced, 1, 2)
    first = low * group_rows + row_index * shard_rows
    own = [lax.dynamic_slice_in_dim(value, first, shard_rows, 0) for value in (upper, upper_next)]
    return jnp.stack(own), diagonals


def solution(mesh):
    return jax.shard_map(
        local,
        mesh=mesh,
        in_specs=(
            P("row", "col"),
            P(),
            P(),
            P(None, ("col", "row"), None),
            P(),
            P(None, "row", "col"),
        ),
        out_specs=(P(None, ("col", "row"), None), P(None, "row", "col")),
        check_vma=False,
    )
```

```python
import jax
import jax.numpy as jnp
from jax import lax
from jax.sharding import PartitionSpec as P


BLK = 128


def swap(value, row_step, col_step):
    rows = lax.axis_size("row")
    cols = lax.axis_size("col")
    if col_step == 0:
        return lax.ppermute(value, "row", [(i, i ^ row_step) for i in range(rows)])
    if row_step == 0:
        return lax.ppermute(value, "col", [(i, i ^ col_step) for i in range(cols)])
    pairs = [
        (row * cols + col, (row ^ row_step) * cols + (col ^ col_step))
        for row in range(rows)
        for col in range(cols)
    ]
    return lax.ppermute(value, ("row", "col"), pairs)


def join(parts, other):
    return jnp.stack([parts, other], axis=1).reshape((-1,) + parts.shape[1:])


def after(value, *others):
    return lax.optimization_barrier((value,) + others)[1:]


def direct_gather(value, others):
    rows = lax.axis_size("row")
    far = {(0, 0): value}
    for j in range(rows - 2, -1, -2):
        for k in (1, 0):
            if j or k:
                far[j, k] = swap(value, j, k)
    far = jnp.stack([jnp.stack([far[j, k] for k in range(2)]) for j in range(0, rows, 2)])
    far, *others = lax.optimization_barrier((far, *others))
    return join(far, swap(far, 1, 0)), others


def rows_first(value):
    rows = lax.axis_size("row")
    far = value[None]
    step = rows // 2
    while step > 1:
        far = join(far, swap(far, step, 0))
        step //= 2
    far = jnp.stack([far, swap(far, 0, 1)], axis=1)
    return join(far, swap(far, 1, 0))


def column_first(value):
    rows = lax.axis_size("row")
    far = jnp.stack([value, swap(value, 0, 1)])[None]
    step = rows // 2
    while step > 1:
        far = join(far, swap(far, step, 0))
        step //= 2
    return join(far, swap(far, 1, 0))


def pick(value, *index):
    sizes = (1,) * len(index) + value.shape[len(index) :]
    start = tuple(index) + (0,) * (value.ndim - len(index))
    return lax.dynamic_slice(value, start, sizes).reshape(value.shape[len(index) :])


def dot(left, right, left_dim=1, right_dim=0):
    return lax.dot_general(
        left,
        right,
        (((left_dim,), (right_dim,)), ((), ())),
        precision=lax.Precision.HIGH,
        preferred_element_type=jnp.float32,
    )


def local(ancestor_inverse, pattern, listed, panels, parent_panels, diag_inverse):
    rows_here, cols_here = ancestor_inverse.shape
    row_count = lax.axis_size("row")
    col_count = lax.axis_size("col")
    row_index = lax.axis_index("row")
    col_index = lax.axis_index("col")
    low = col_index % 2
    high = col_index // 2
    planes = col_count // 2
    super_count, shard_rows, width = panels.shape
    tile_rows = width // row_count
    tile_cols = width // col_count
    group_rows = row_count * shard_rows
    plane_rows = 2 * group_rows
    blocks = pattern.shape[0]
    assert super_count == 2 and planes == row_count and rows_here == plane_rows
    assert group_rows == cols_here == BLK and blocks == col_count
    assert 2 * shard_rows == tile_cols
    members = [
        [(2 * plane + near) * row_count + row for near in range(2) for row in range(row_count)]
        for plane in range(planes)
    ]

    held = rows_first(ancestor_inverse)

    shares = jnp.swapaxes(panels.reshape(2, shard_rows, row_count, tile_rows), 1, 2)
    shares = shares.reshape(2 * row_count, shard_rows, tile_rows)
    piece = lax.all_to_all(
        shares, ("col", "row"), 0, 0, tiled=True, axis_index_groups=members
    ).reshape(plane_rows, tile_rows)

    pieces = {0: piece}
    step = planes // 2
    while step:
        for j in list(pieces):
            pieces[j ^ step] = swap(pieces[j], 0, 2 * step)
        step //= 2
    pattern, listed, link = after(pieces[planes // 2], pattern, listed, parent_panels[0])

    block_ids = jnp.arange(blocks, dtype=jnp.int32)
    flags = jnp.any(listed[:, :, None] == block_ids[None, None, :], axis=1).astype(jnp.float32)
    seen = lax.dynamic_slice_in_dim(pattern, 2 * high, 2, 1).astype(jnp.float32)
    seen = (seen * pick(flags, low)[:, None]).reshape(planes, 2, 2)
    order = sorted(pieces, key=lambda j: (bin(j).count("1"), -j))
    early = [j for j in order if bin(j).count("1") < 2]
    late = [j for j in order if bin(j).count("1") > 1]
    total = None
    for group in (early, late):
        left = []
        for j in group:
            source = high ^ j
            weights = [
                pick(held, row_index ^ source, low ^ near).reshape(2, BLK, cols_here)
                * pick(seen, source)[:, near][:, None, None]
                for near in range(2)
            ]
            left.append(
                jnp.concatenate([value.reshape(plane_rows, cols_here) for value in weights], axis=1)
            )
        left = jnp.concatenate(left, axis=0)
        right = jnp.concatenate([pieces[j] for j in group], axis=0)
        term = dot(left, right, 0, 0)
        total = term if total is None else total + term

    keep = lax.dynamic_slice_in_dim(flags, 2 * high, 2, 1)
    keep = jnp.repeat(keep, BLK, axis=1)[:, :, None]
    raw = jnp.concatenate([panels.reshape(2 * shard_rows, width), diag_inverse[0].T], axis=1)
    raw = column_first(raw)
    raw = jnp.stack([pick(raw, row_index ^ r, low ^ k) for k in range(2) for r in range(row_count)])
    diag_rows = raw[:, :, width:].reshape(2, row_count, tile_cols, tile_rows)
    diag_rows = jnp.concatenate(
        [diag_rows[:, r].reshape(2 * tile_cols, tile_rows) for r in range(row_count)], axis=1
    )
    kept_all = [
        raw[:, s * shard_rows : (s + 1) * shard_rows, :width].reshape(plane_rows, width) * keep[s]
        for s in range(2)
    ]

    def band(value):
        return lax.dynamic_slice_in_dim(value, row_index * tile_rows, tile_rows, 1)

    kept_own = [band(value) for value in kept_all]
    link_own = band(link)
    moved = dot(kept_all[0], link_own)
    link_rows = lax.dynamic_slice_in_dim(link, high * 2 * tile_cols, 2 * tile_cols, 0)
    base = dot(dot(diag_rows, link_own), link_rows, 0, 0)

    sums, (moved, base, kept_next, first_own, next_own, link) = direct_gather(
        total, (moved, base, kept_all[1], kept_own[0], kept_own[1], link)
    )
    sums = [
        jnp.concatenate([pick(sums, row_index ^ r, low ^ s) for r in range(row_count)], axis=1)
        for s in range(2)
    ]
    upper = -sums[0] * keep[0]
    chained = dot(upper, link)
    upper_next = -(sums[1] + chained) * keep[1]
    tiles = [
        lax.optimization_barrier(dot(first_own, -upper, 0, 0)),
        base
        + dot(next_own, -upper_next, 0, 0)
        + dot(band(chained), kept_next, 0, 0)
        + dot(-moved, chained, 0, 0),
    ]
    tiles = jnp.stack([tile.T for tile in tiles]).reshape(2, planes, 2, tile_cols, tile_rows)
    tiles = lax.dynamic_index_in_dim(tiles, low, 2, keepdims=False)
    reduced = lax.dynamic_index_in_dim(tiles, high, 1, keepdims=False)
    for j in range(planes - 1, 0, -1):
        tile = lax.dynamic_index_in_dim(tiles, high ^ j, 1, keepdims=False)
        reduced = reduced + swap(tile, 0, 2 * j)
    diagonals = diag_inverse + jnp.swapaxes(reduced, 1, 2)
    first = low * group_rows + row_index * shard_rows
    own = [lax.dynamic_slice_in_dim(value, first, shard_rows, 0) for value in (upper, upper_next)]
    return jnp.stack(own), diagonals


def solution(mesh):
    return jax.shard_map(
        local,
        mesh=mesh,
        in_specs=(
            P("row", "col"),
            P(),
            P(),
            P(None, ("col", "row"), None),
            P(),
            P(None, "row", "col"),
        ),
        out_specs=(P(None, ("col", "row"), None), P(None, "row", "col")),
        check_vma=False,
    )
```
